32 devices in a mesh: row: 2 (over x), col: 16 (over z, y, core).
Axes of the slice: x: 2, y: 2, z: 4, core: 2. Of those that a mesh axis runs over, the one named last changes fastest.
Arguments:
- src_pos: float32 [3, 8192], P(None, 'row'), may hold values from 0 to 1
- src_desc: bfloat16 [64, 8192], P(None, 'row'), may hold values from -2.5 to 2.5
- src_mass: float32 [8192], P('row'), may hold values from 0.2 to 5
- tgt_pos: float32 [3, 8192], P(None, 'col'), may hold values from 0 to 1
- tgt_desc: bfloat16 [64, 8192], P(None, 'col'), may hold values from -2.5 to 2.5
- tgt_mass: float32 [8192], P('col'), may hold values from 0.2 to 5
- pattern: int32 [64, 20], P('row'), may hold values from 0 to 63, all different within a row
Outputs:
- row_potential: float32 [8192], P('row')
- col_potential: float32 [8192], P('col')
- mapped_desc: float32 [8192, 64], P(('row', 'col'))
The draws below stay inside these ranges and needn't reach their ends.
Inputs may be any that keep to these rules, and one draw needn't show every extreme that they name: `pattern`: each row names 20 different target clusters, and every target cluster is named by some row.
All inputs are finite; a program needn't handle non-finite values.
Results may differ from the reference program's by a relative error of at most 0.0028.
Values may be sent and summed in bfloat16 or wider, within the bound.
A program may use at most 64 MiB of HBM per device.

```python
import math
import jax
import jax.numpy as jnp
from jax import lax

CL = 128
F = 64
TOP = 20
ITERS = 2
NSC = 64
NTC = 64
NS = 8192
NT = 8192


def shared_direction(key):
    flips = jax.random.bernoulli(jax.random.fold_in(key, 7001), 0.5, (F,))
    return jnp.where(flips, 1.0, -1.0).astype(jnp.float32) / jnp.sqrt(jnp.float32(F))


def draw_src_desc(key, part):
    direction = shared_direction(key)
    values = jax.random.truncated_normal(jax.random.fold_in(key, 11), -4.0, 4.0, (F, NSC * CL), jnp.float32) * 0.125
    index = jnp.arange(NSC * CL)
    level = 2.5 + 0.5 * (index // 61 % 3).astype(jnp.float32)
    along = jnp.where(index % 61 == 7, level, 0.0)
    values = jnp.clip(values + direction[:, None] * along[None, :], -2.5, 2.5)
    return values.astype(jnp.bfloat16)


def draw_tgt_desc(key, part):
    direction = shared_direction(key)
    values = jax.random.truncated_normal(jax.random.fold_in(key, 13), -4.0, 4.0, (F, NTC * CL), jnp.float32) * 0.125
    index = jnp.arange(NTC * CL)
    level = 1.5 + 0.5 * (index // 7 % 5).astype(jnp.float32)
    along = jnp.where(index % 7 == 3, level, 0.0)
    values = jnp.clip(values + direction[:, None] * along[None, :], -2.5, 2.5)
    return values.astype(jnp.bfloat16)


def levels(key, extent, cuts, least, top_value):
    level, own = 1.0, jax.random.fold_in(key, 6)
    for position, blocks in cuts:
        draws = jnp.exp(jax.random.uniform(jax.random.fold_in(own, position), (blocks,), jnp.float32, least / len(cuts), top_value / len(cuts)))
        level = level * jnp.repeat(draws, extent[position] // blocks).reshape([-1 if axis == position else 1 for axis in range(len(extent))])
    return level


def distinct(key, rows, number_of, top, lift):
    sequence = jax.random.permutation(jax.random.fold_in(key, 1), number_of)
    pull = sequence
    for power in range(3):
        pull = pull * pull // number_of
    pull = pull * lift // number_of
    tickets = jax.random.randint(jax.random.fold_in(key, 2), (rows, number_of), 0, 4096) + pull
    holders = jax.random.permutation(jax.random.fold_in(key, 3), rows)[jnp.arange(number_of) % rows]
    tickets = jnp.where(jnp.arange(rows)[:, None] == holders[None, :], 1 << 14, tickets)
    merit = tickets * number_of + jnp.arange(number_of)
    return lax.top_k(merit.astype(jnp.int32), top)[1].astype(jnp.int32)


def setup_inputs(seed: int = 0) -> dict:
    keys = jax.random.split(jax.random.key(seed), 8)
    return {
        "src_pos": jnp.clip(1.0 * jax.random.uniform(keys[0], (3, NS), jnp.float32) ** levels(keys[0], (3, NS), ((1, 2),), -0.2, 0.2), 0.0, 1.0),
        "src_desc": draw_src_desc(jax.random.fold_in(keys[7], 71), 0),
        "src_mass": jnp.clip(jnp.exp(math.log(5.0) - 3.218876 * jax.random.uniform(keys[2], (NS,), jnp.float32) ** levels(keys[2], (NS,), ((0, 2),), -0.2, 0.2)), 0.2, 5.0),
        "tgt_pos": jnp.clip(1.0 * jax.random.uniform(keys[3], (3, NT), jnp.float32) ** levels(keys[3], (3, NT), ((1, 16),), -0.2, 0.2), 0.0, 1.0),
        "tgt_desc": draw_tgt_desc(jax.random.fold_in(keys[7], 71), 0),
        "tgt_mass": jnp.clip(jnp.exp(math.log(5.0) - 3.218876 * jax.random.uniform(keys[5], (NT,), jnp.float32) ** levels(keys[5], (NT,), ((0, 16),), -0.2, 0.2)), 0.2, 5.0),
        "pattern": distinct(keys[6], NSC, NTC, TOP, 2560),
    }


EPSILON = 0.05
PRECISE = lax.Precision.HIGHEST


def cluster_costs(item, tgt_pos3, tgt_desc3, tgt_norm):
    own_pos, own_desc, target_ids = item[0], item[1], item[2]
    near_pos = tgt_pos3[target_ids]
    near_desc = tgt_desc3[target_ids]
    inner = jnp.einsum('fa,jfb->jab', own_desc, near_desc, precision=PRECISE)
    inner = inner + jnp.einsum('ka,jkb->jab', own_pos, near_pos, precision=PRECISE)
    return tgt_norm[target_ids][:, None, :] - 2.0 * inner


def reference(src_pos, src_desc, src_mass, tgt_pos, tgt_desc, tgt_mass, pattern):
    src_clusters = pattern.shape[0]
    tgt_clusters = tgt_pos.shape[1] // CL
    desc_src = src_desc.astype(jnp.float32)
    desc_tgt = tgt_desc.astype(jnp.float32)
    tgt_norm = (jnp.sum(tgt_pos * tgt_pos, axis=0) + jnp.sum(desc_tgt * desc_tgt, axis=0)).reshape(tgt_clusters, CL)
    src_pos3 = src_pos.reshape(3, src_clusters, CL).transpose(1, 0, 2)
    src_desc3 = desc_src.reshape(F, src_clusters, CL).transpose(1, 0, 2)
    tgt_pos3 = tgt_pos.reshape(3, tgt_clusters, CL).transpose(1, 0, 2)
    tgt_desc3 = desc_tgt.reshape(F, tgt_clusters, CL).transpose(1, 0, 2)
    log_src = jnp.log(src_mass).reshape(src_clusters, CL)
    log_tgt = jnp.log(tgt_mass).reshape(tgt_clusters, CL)
    blocks = (src_pos3, src_desc3, pattern)

    def row_scores(item, col_pot):
        return (col_pot[item[2]][:, None, :] - cluster_costs(item, tgt_pos3, tgt_desc3, tgt_norm)) / EPSILON

    def col_scores(item):
        return (item[3][None, :, None] - cluster_costs(item, tgt_pos3, tgt_desc3, tgt_norm)) / EPSILON

    def update_rows(col_pot):
        def row_lse(item):
            scores = row_scores(item, col_pot)
            row_peak = jnp.max(scores, axis=(0, 2))
            return row_peak + jnp.log(jnp.sum(jnp.exp(scores - row_peak[None, :, None]), axis=(0, 2)))
        return EPSILON * log_src - EPSILON * lax.map(row_lse, blocks)

    def update_cols(row_pot):
        with_rows = blocks + (row_pot,)

        def tile_peak(item):
            return jnp.max(col_scores(item), axis=1)

        col_peak = jnp.full((tgt_clusters, CL), -jnp.inf, jnp.float32).at[pattern].max(lax.map(tile_peak, with_rows))

        def col_part(item):
            return jnp.sum(jnp.exp(col_scores(item) - col_peak[item[2]][:, None, :]), axis=1)

        col_total = jnp.zeros((tgt_clusters, CL), jnp.float32).at[pattern].add(lax.map(col_part, with_rows))
        return EPSILON * log_tgt - EPSILON * (col_peak + jnp.log(col_total))

    col_pot = jnp.zeros((tgt_clusters, CL), jnp.float32)
    row_pot = jnp.zeros((src_clusters, CL), jnp.float32)
    for iteration in range(ITERS):
        row_pot = update_rows(col_pot)
        col_pot = update_cols(row_pot)

    def mapped_rows(item):
        scores = row_scores(item, col_pot)
        row_peak = jnp.max(scores, axis=(0, 2))
        weight = jnp.exp(scores - row_peak[None, :, None])
        den_sum = jnp.sum(weight, axis=(0, 2))
        rounded = lax.optimization_barrier(weight.astype(jnp.bfloat16)).astype(jnp.float32)
        num_sum = jnp.einsum('jab,jfb->af', rounded, tgt_desc3[item[2]], precision=PRECISE)
        return num_sum / den_sum[:, None]

    mapped = lax.map(mapped_rows, blocks).reshape(src_clusters * CL, F)
    return row_pot.reshape(-1), col_pot.reshape(-1), mapped
```

```python
import functools
import math

import jax
import jax.numpy as jnp
from jax import lax
from jax.experimental import pallas as pl
from jax.experimental.pallas import tpu as pltpu
from jax.sharding import PartitionSpec as P

CL = 128
EPSILON = 0.05
LOG2E = 1.0 / math.log(2.0)
SCORE_SCALE = 2.0 * LOG2E / EPSILON
POT_SCALE = EPSILON * math.log(2.0)
MASKED = -(2.0**93)
MESH = pl.DeviceIdType.MESH
NUM_ROWS = 16


def log2(value):
    return jnp.log(value) * LOG2E


def float_parts(value):
    first = value.astype(jnp.bfloat16).astype(jnp.float32)
    rest = value - first
    second = rest.astype(jnp.bfloat16).astype(jnp.float32)
    return first, second, (rest - second).astype(jnp.bfloat16).astype(jnp.float32)


def hi_lo(value):
    high = value.astype(jnp.bfloat16)
    low = (value - high.astype(jnp.float32)).astype(jnp.bfloat16)
    return high, low


def hi_lo_rows(value):
    high = value.astype(jnp.bfloat16).astype(jnp.float32)
    low = value - high
    row = lax.broadcasted_iota(jnp.int32, (NUM_ROWS, value.shape[1]), 0)
    rows = jnp.where(row == 0, high, jnp.where(row == 1, low, 0.0))
    return rows.astype(jnp.bfloat16)


def kernel(
    n_row, n_col,
    src_pos_ref, src_desc_ref, src_mask_ref, src_mass_ref, tgt_pos_ref, desc_ref, tgt_mass_ref,
    row_out, col_out, map_out,
    src_feat, tgt_feat, score, plan, stat_send, stat_recv, rp_all, col_max, col_sum, col_stat, sum_send, sum_recv, u_all,
    col_part, num_send, num_recv,
    stat_ss, stat_rs, rp_ss, rp_rs, cs_ss, cs_rs, sum_ss, sum_rs, u_ss, u_rs, cp_ss, cp_rs, num_ss, num_rs,
):
    me = lax.axis_index("col")
    mine = lax.axis_index("row")
    n_tgt = desc_ref.shape[1]
    width = map_out.shape[1]
    fold = min(width, 128)
    n_feat = desc_ref.shape[0]

    def col_peer(offset):
        return lax.rem(me + offset, n_col)

    def row_peer(offset):
        return lax.rem(mine + offset, n_row)

    barrier = pltpu.get_barrier_semaphore()

    @pl.loop(1, n_col)
    def _(offset):
        pl.semaphore_signal(barrier, inc=1, device_id={"col": col_peer(offset)}, device_id_type=MESH)

    @pl.loop(1, n_row)
    def _(offset):
        pl.semaphore_signal(barrier, inc=1, device_id={"row": row_peer(offset)}, device_id_type=MESH)

    def to_owner(send, recv, ssem, rsem, peer):
        return pltpu.make_async_remote_copy(
            src_ref=send.at[peer], dst_ref=recv.at[me], send_sem=ssem.at[peer], recv_sem=rsem.at[me],
            device_id={"col": peer}, device_id_type=MESH,
        )

    def from_peer(send, recv, ssem, rsem, peer):
        return pltpu.make_async_remote_copy(
            src_ref=send.at[peer], dst_ref=recv.at[peer], send_sem=ssem.at[peer], recv_sem=rsem.at[peer],
            device_id={"col": peer}, device_id_type=MESH,
        )

    def spread(buf, ssem, rsem, peer):
        return pltpu.make_async_remote_copy(
            src_ref=buf.at[me], dst_ref=buf.at[me], send_sem=ssem.at[peer], recv_sem=rsem.at[me],
            device_id={"col": peer}, device_id_type=MESH,
        )

    def spread_from(buf, ssem, rsem, peer):
        return pltpu.make_async_remote_copy(
            src_ref=buf.at[me], dst_ref=buf.at[peer], send_sem=ssem.at[peer], recv_sem=rsem.at[peer],
            device_id={"col": peer}, device_id_type=MESH,
        )

    def row_spread(buf, ssem, rsem, peer):
        return pltpu.make_async_remote_copy(
            src_ref=buf.at[mine], dst_ref=buf.at[mine], send_sem=ssem.at[peer], recv_sem=rsem.at[mine],
            device_id={"row": peer}, device_id_type=MESH,
        )

    def row_spread_from(buf, ssem, rsem, peer):
        return pltpu.make_async_remote_copy(
            src_ref=buf.at[mine], dst_ref=buf.at[peer], send_sem=ssem.at[peer], recv_sem=rsem.at[peer],
            device_id={"row": peer}, device_id_type=MESH,
        )

    def block_of(ref, block):
        if ref.ndim == 3:
            return ref[block]
        return ref[:, pl.ds(pl.multiple_of(block * width, 128), width)]

    desc32 = desc_ref[...].astype(jnp.float32)
    tgt_pos = tgt_pos_ref[...]
    norm = jnp.sum(tgt_pos * tgt_pos, axis=0, keepdims=True) + jnp.sum(desc32 * desc32, axis=0, keepdims=True)
    n_mask = src_mask_ref.shape[-2]
    lane = lax.broadcasted_iota(jnp.int32, (n_mask, n_tgt), 1) // CL
    in_cluster = lane == lax.broadcasted_iota(jnp.int32, (n_mask, n_tgt), 0)
    t1, t2, t3 = float_parts(jnp.concatenate([tgt_pos, -0.5 * norm, jnp.where(in_cluster, 1.0, 0.0)], axis=0))
    tgt_feat[...] = jnp.concatenate([desc32, t1, t2, t1, t2, t3, t1], axis=0).T.astype(jnp.bfloat16)
    ones = jnp.ones((1, width), jnp.float32)

    def row_stat(block):
        s1, s2, s3 = float_parts(
            jnp.concatenate([block_of(src_pos_ref, block), ones, block_of(src_mask_ref, block)], axis=0)
        )
        src_feat[0:n_feat, :] = block_of(src_desc_ref, block)
        src_feat[n_feat:, :] = jnp.concatenate([s1, s1, s2, s2, s1, s3], axis=0).astype(jnp.bfloat16)
        score[block] = SCORE_SCALE * jnp.dot(
            tgt_feat[...], src_feat[...], preferred_element_type=jnp.float32
        )
        peak = jnp.max(score[block], axis=0, keepdims=True)
        total = jnp.sum(jnp.exp2(score[block] - peak), axis=0, keepdims=True)
        return peak, total

    peak, total = row_stat(me)
    stat_recv[me, 0:1, :] = peak
    stat_recv[me, 1:2, :] = total
    pl.semaphore_wait(barrier, n_col - 1 + n_row - 1)

    @pl.loop(1, n_col)
    def _(offset):
        peer = col_peer(offset)
        peak, total = row_stat(peer)
        stat_send[peer, 0:1, :] = peak
        stat_send[peer, 1:2, :] = total
        to_owner(stat_send, stat_recv, stat_ss, stat_rs, peer).start()

    @pl.loop(1, n_col)
    def _(offset):
        from_peer(stat_send, stat_recv, stat_ss, stat_rs, col_peer(offset)).wait()

    peaks = stat_recv[:, 0:1, :]
    top = jnp.max(peaks, axis=0, keepdims=True)
    row_total = jnp.sum(stat_recv[:, 1:2, :] * jnp.exp2(peaks - top), axis=0)
    own_mass = block_of(src_mass_ref, me)
    rp_all[me] = log2(own_mass) - (top[0] + log2(row_total))

    @pl.loop(1, n_col)
    def _(offset):
        spread(rp_all, rp_ss, rp_rs, col_peer(offset)).start()

    @pl.loop(1, n_col)
    def _(offset):
        spread_from(rp_all, rp_ss, rp_rs, col_peer(offset)).wait()

    strip = 64

    def folded(value, join):
        parts = [value[:, at : at + fold] for at in range(0, width, fold)]
        return functools.reduce(join, parts)

    @pl.loop(0, n_tgt // strip)
    def _(index):
        rows = pl.ds(pl.multiple_of(index * strip, strip), strip)

        def highest(block, running):
            return jnp.maximum(running, folded(score[block, rows, :] + rp_all[block], jnp.maximum))

        running = lax.fori_loop(0, n_col, highest, jnp.full((strip, fold), -3e38, jnp.float32), unroll=4)
        col_max[rows, :] = running
        peak = jnp.max(running, axis=1, keepdims=True)

        def summed(block, running):
            part = jnp.exp2(score[block, rows, :] + (rp_all[block] - peak))
            plan[block, rows, :] = part.astype(jnp.bfloat16)
            return running + folded(part, jnp.add)

        col_sum[rows, :] = lax.fori_loop(0, n_col, summed, jnp.zeros((strip, fold), jnp.float32), unroll=4)

    own_peak = jnp.max(col_max[...].T, axis=0, keepdims=True)
    col_stat[mine, 0:1, :] = own_peak
    col_stat[mine, 1:2, :] = jnp.sum(col_sum[...].T, axis=0, keepdims=True)

    @pl.loop(1, n_row)
    def _(offset):
        row_spread(col_stat, cs_ss, cs_rs, row_peer(offset)).start()

    @pl.loop(1, n_row)
    def _(offset):
        row_spread_from(col_stat, cs_ss, cs_rs, row_peer(offset)).wait()

    peaks = col_stat[:, 0:1, :]
    top = jnp.max(peaks, axis=0, keepdims=True)
    col_total = jnp.sum(col_stat[:, 1:2, :] * jnp.exp2(peaks - top), axis=0)
    tgt_mass = tgt_mass_ref[...]
    col_pot = log2(tgt_mass) - (top[0] + log2(col_total))
    gain = jnp.exp2(own_peak + col_pot)

    gain_rows = hi_lo_rows(gain)

    def row_sum(block):
        rows = jnp.dot(gain_rows, plan[block], preferred_element_type=jnp.float32)
        return rows[0:1] + rows[1:2]

    @pl.loop(1, n_col)
    def _(offset):
        peer = col_peer(offset)
        sum_send[peer] = row_sum(peer)
        to_owner(sum_send, sum_recv, sum_ss, sum_rs, peer).start()

    sum_recv[me] = row_sum(me)

    @pl.loop(1, n_col)
    def _(offset):
        from_peer(sum_send, sum_recv, sum_ss, sum_rs, col_peer(offset)).wait()

    u_all[me] = own_mass / jnp.sum(sum_recv[...], axis=0)

    @pl.loop(1, n_col)
    def _(offset):
        spread(u_all, u_ss, u_rs, col_peer(offset)).start()

    @pl.loop(1, n_col)
    def _(offset):
        spread_from(u_all, u_ss, u_rs, col_peer(offset)).wait()

    def col_add(block, running):
        return running + lax.dot_general(
            hi_lo_rows(u_all[block]), plan[block], (((1,), (1,)), ((), ())), preferred_element_type=jnp.float32
        )

    both = lax.fori_loop(0, n_col, col_add, jnp.zeros((NUM_ROWS, n_tgt), jnp.float32))
    col_part[mine] = gain * (both[0:1] + both[1:2])

    @pl.loop(1, n_row)
    def _(offset):
        row_spread(col_part, cp_ss, cp_rs, row_peer(offset)).start()

    for block in range(n_col):
        row_out[:, block * width : (block + 1) * width] = POT_SCALE * (rp_all[block] + log2(u_all[block]))

    @pl.loop(1, n_row)
    def _(offset):
        row_spread_from(col_part, cp_ss, cp_rs, row_peer(offset)).wait()

    ratio = tgt_mass / jnp.sum(col_part[...], axis=0)
    col_out[...] = POT_SCALE * (col_pot + log2(ratio))
    factor = gain * ratio
    weighted_high, weighted_low = hi_lo(desc_ref[...].astype(jnp.float32) * factor)
    weights = jnp.concatenate([weighted_high, hi_lo_rows(factor), weighted_low], axis=0)

    def image(block):
        sums = jnp.dot(weights, plan[block], preferred_element_type=jnp.float32)
        den = sums[n_feat : n_feat + 1] + sums[n_feat + 1 : n_feat + 2]
        num = sums[:n_feat] + sums[n_feat + NUM_ROWS :]
        return jnp.concatenate([num.astype(jnp.bfloat16), hi_lo_rows(den)], axis=0)

    @pl.loop(1, n_col)
    def _(offset):
        peer = col_peer(offset)
        num_send[peer] = image(peer)
        to_owner(num_send, num_recv, num_ss, num_rs, peer).start()

    num_recv[me] = image(me)

    @pl.loop(1, n_col)
    def _(offset):
        from_peer(num_send, num_recv, num_ss, num_rs, col_peer(offset)).wait()

    def add(block, running):
        return running + num_recv[block].astype(jnp.float32)

    sums = lax.fori_loop(0, n_col, add, jnp.zeros((n_feat + NUM_ROWS, width), jnp.float32))
    den = sums[n_feat : n_feat + 1] + sums[n_feat + 1 : n_feat + 2]
    map_out[...] = sums[:n_feat] / den


def on_device(n_row, n_col, src_pos, src_desc, src_mass, tgt_pos, tgt_desc, tgt_mass, pattern):
    n_src = src_pos.shape[1]
    n_tgt = tgt_pos.shape[1]
    n_feat = src_desc.shape[0]
    tgt_clusters = n_tgt // CL
    width = n_src // n_col
    column = lax.axis_index("col")
    own = column * tgt_clusters + jnp.arange(tgt_clusters, dtype=jnp.int32)
    named = jnp.any(pattern[None, :, :] == own[:, None, None], axis=2)
    named = jnp.broadcast_to(named[:, :, None], named.shape + (CL,)).reshape(tgt_clusters, n_src)
    n_mask = -(-(4 + tgt_clusters) // 8) * 8 - 4
    src_mask = jnp.where(jnp.pad(named, ((0, n_mask - tgt_clusters), (0, 0)), constant_values=True), 0.0, MASKED)
    depth = n_feat + 6 * (4 + n_mask)

    def blocked(value):
        if width % 128 == 0:
            return value
        return value.reshape(value.shape[0], n_col, width).transpose(1, 0, 2)

    f32, bf16 = jnp.float32, jnp.bfloat16
    vmem = pl.BlockSpec(memory_space=pltpu.VMEM)
    fold = min(width, 128)
    tall = n_feat + NUM_ROWS
    dma = pltpu.SemaphoreType.DMA
    row_pot, col_pot, mapped = pl.pallas_call(
        functools.partial(kernel, n_row, n_col),
        out_shape=(
            jax.ShapeDtypeStruct((1, n_src), f32),
            jax.ShapeDtypeStruct((1, n_tgt), f32),
            jax.ShapeDtypeStruct((n_feat, width), f32),
        ),
        in_specs=[vmem] * 7,
        out_specs=(vmem, vmem, vmem),
        scratch_shapes=[
            pltpu.VMEM((depth, width), bf16),
            pltpu.VMEM((n_tgt, depth), bf16),
            pltpu.VMEM((n_col, n_tgt, width), f32),
            pltpu.VMEM((n_col, n_tgt, width), bf16),
            pltpu.VMEM((n_col, 2, width), f32),
            pltpu.VMEM((n_col, 2, width), f32),
            pltpu.VMEM((n_col, 1, width), f32),
            pltpu.VMEM((n_tgt, fold), f32),
            pltpu.VMEM((n_tgt, fold), f32),
            pltpu.VMEM((n_row, 2, n_tgt), f32),
            pltpu.VMEM((n_col, 1, width), f32),
            pltpu.VMEM((n_col, 1, width), f32),
            pltpu.VMEM((n_col, 1, width), f32),
            pltpu.VMEM((n_row, 1, n_tgt), f32),
            pltpu.VMEM((n_col, tall, width), bf16),
            pltpu.VMEM((n_col, tall, width), bf16),
            dma((n_col,)), dma((n_col,)),
            dma((n_col,)), dma((n_col,)),
            dma((n_row,)), dma((n_row,)),
            dma((n_col,)), dma((n_col,)),
            dma((n_col,)), dma((n_col,)),
            dma((n_row,)), dma((n_row,)),
            dma((n_col,)), dma((n_col,)),
        ],
        compiler_params=pltpu.CompilerParams(
            collective_id=0, has_side_effects=True, vmem_limit_bytes=56 * 1024 * 1024
        ),
    )(
        blocked(src_pos), blocked(src_desc), blocked(src_mask), blocked(src_mass.reshape(1, n_src)),
        tgt_pos, tgt_desc, tgt_mass.reshape(1, n_tgt),
    )
    return (row_pot.reshape(-1), col_pot.reshape(-1), mapped.T)


def solution(mesh):
    in_specs = (
        P(None, "row"),
        P(None, "row"),
        P("row"),
        P(None, "col"),
        P(None, "col"),
        P("col"),
        P("row", None),
    )
    out_specs = (P("row"), P("col"), P(("row", "col"), None))
    body = functools.partial(on_device, mesh.shape["row"], mesh.shape["col"])
    return jax.shard_map(body, mesh=mesh, in_specs=in_specs, out_specs=out_specs, check_vma=False)
```

```python
import functools
import math

import jax
import jax.numpy as jnp
from jax import lax
from jax.experimental import pallas as pl
from jax.experimental.pallas import tpu as pltpu
from jax.sharding import PartitionSpec as P

CL = 128
EPSILON = 0.05
LOG2E = 1.0 / math.log(2.0)
SCORE_SCALE = 2.0 * LOG2E / EPSILON
POT_SCALE = EPSILON * math.log(2.0)
MASKED = -(2.0**93)
MESH = pl.DeviceIdType.MESH
NUM_ROWS = 16


def log2(value):
    return jnp.log(value) * LOG2E


def float_parts(value):
    first = value.astype(jnp.bfloat16).astype(jnp.float32)
    rest = value - first
    second = rest.astype(jnp.bfloat16).astype(jnp.float32)
    return first, second, (rest - second).astype(jnp.bfloat16).astype(jnp.float32)


def hi_lo(value):
    high = value.astype(jnp.bfloat16)
    low = (value - high.astype(jnp.float32)).astype(jnp.bfloat16)
    return high, low


def hi_lo_rows(value):
    high = value.astype(jnp.bfloat16).astype(jnp.float32)
    low = value - high
    row = lax.broadcasted_iota(jnp.int32, (NUM_ROWS, value.shape[1]), 0)
    rows = jnp.where(row == 0, high, jnp.where(row == 1, low, 0.0))
    return rows.astype(jnp.bfloat16)


def flipped(place, mask, count):
    bits = count.bit_length() - 1
    if count != 1 << bits:
        return lax.rem(place + mask, count)
    digits = [lax.rem(lax.div(place, 1 << bit) + lax.div(mask, 1 << bit), 2) for bit in range(bits)]
    return sum(digit * (1 << bit) for bit, digit in enumerate(digits))


def kernel(
    n_row, n_col,
    src_pos_ref, src_desc_ref, src_mask_ref, src_mass_ref, tgt_pos_ref, desc_ref, tgt_mass_ref,
    row_out, col_out, map_out,
    src_feat, tgt_feat, score, plan, stat_send, stat_recv, rp_all, col_max, col_sum, col_stat, sum_send, sum_recv, u_all,
    col_part, pair_send, pair_recv, num_send, num_recv, den_send, den_recv,
    stat_ss, stat_rs, rp_ss, rp_rs, cs_ss, cs_rs, sum_ss, sum_rs, u_ss, u_rs, cp_ss, cp_rs, pair_ss, pair_rs, num_ss, num_rs, den_ss, den_rs,
):
    me = lax.axis_index("col")
    mine = lax.axis_index("row")
    n_tgt = desc_ref.shape[1]
    width = map_out.shape[1]
    fold = min(width, 128)
    n_feat = desc_ref.shape[0]

    def col_peer(offset):
        return flipped(me, n_col - offset, n_col)

    def row_peer(offset):
        return lax.rem(mine + offset, n_row)

    barrier = pltpu.get_barrier_semaphore()

    @pl.loop(1, n_col)
    def _(offset):
        pl.semaphore_signal(barrier, inc=1, device_id={"col": col_peer(offset)}, device_id_type=MESH)

    @pl.loop(1, n_row)
    def _(offset):
        pl.semaphore_signal(barrier, inc=1, device_id={"row": row_peer(offset)}, device_id_type=MESH)

    def to_owner(send, recv, ssem, rsem, peer):
        return pltpu.make_async_remote_copy(
            src_ref=send.at[peer], dst_ref=recv.at[me], send_sem=ssem.at[peer], recv_sem=rsem.at[me],
            device_id={"col": peer}, device_id_type=MESH,
        )

    def from_peer(send, recv, ssem, rsem, peer):
        return pltpu.make_async_remote_copy(
            src_ref=send.at[peer], dst_ref=recv.at[peer], send_sem=ssem.at[peer], recv_sem=rsem.at[peer],
            device_id={"col": peer}, device_id_type=MESH,
        )

    def spread(buf, ssem, rsem, peer):
        return pltpu.make_async_remote_copy(
            src_ref=buf.at[me], dst_ref=buf.at[me], send_sem=ssem.at[peer], recv_sem=rsem.at[me],
            device_id={"col": peer}, device_id_type=MESH,
        )

    def spread_from(buf, ssem, rsem, peer):
        return pltpu.make_async_remote_copy(
            src_ref=buf.at[me], dst_ref=buf.at[peer], send_sem=ssem.at[peer], recv_sem=rsem.at[peer],
            device_id={"col": peer}, device_id_type=MESH,
        )

    def row_spread(buf, ssem, rsem, peer):
        return pltpu.make_async_remote_copy(
            src_ref=buf.at[mine], dst_ref=buf.at[mine], send_sem=ssem.at[peer], recv_sem=rsem.at[mine],
            device_id={"row": peer}, device_id_type=MESH,
        )

    def row_spread_from(buf, ssem, rsem, peer):
        return pltpu.make_async_remote_copy(
            src_ref=buf.at[mine], dst_ref=buf.at[peer], send_sem=ssem.at[peer], recv_sem=rsem.at[peer],
            device_id={"row": peer}, device_id_type=MESH,
        )

    def block_of(ref, block):
        if ref.ndim == 3:
            return ref[block]
        return ref[:, pl.ds(pl.multiple_of(block * width, 128), width)]

    desc32 = desc_ref[...].astype(jnp.float32)
    tgt_pos = tgt_pos_ref[...]
    norm = jnp.sum(tgt_pos * tgt_pos, axis=0, keepdims=True) + jnp.sum(desc32 * desc32, axis=0, keepdims=True)
    n_mask = src_mask_ref.shape[-2]
    lane = lax.broadcasted_iota(jnp.int32, (n_mask, n_tgt), 1) // CL
    in_cluster = lane == lax.broadcasted_iota(jnp.int32, (n_mask, n_tgt), 0)
    t1, t2, t3 = float_parts(jnp.concatenate([tgt_pos, -0.5 * norm, jnp.where(in_cluster, 1.0, 0.0)], axis=0))
    tgt_feat[...] = jnp.concatenate([desc32, t1, t2, t1, t2, t3, t1], axis=0).T.astype(jnp.bfloat16)
    ones = jnp.ones((1, width), jnp.float32)

    def row_stat(block):
        s1, s2, s3 = float_parts(
            jnp.concatenate([block_of(src_pos_ref, block), ones, block_of(src_mask_ref, block)], axis=0)
        )
        src_feat[0:n_feat, :] = block_of(src_desc_ref, block)
        src_feat[n_feat:, :] = jnp.concatenate([s1, s1, s2, s2, s1, s3], axis=0).astype(jnp.bfloat16)
        score[block] = SCORE_SCALE * jnp.dot(
            tgt_feat[...], src_feat[...], preferred_element_type=jnp.float32
        )
        peak = jnp.max(score[block], axis=0, keepdims=True)
        total = jnp.sum(jnp.exp2(score[block] - peak), axis=0, keepdims=True)
        return peak, total

    peak, total = row_stat(me)
    stat_recv[me, 0:1, :] = peak
    stat_recv[me, 1:2, :] = total
    early = n_col // 2

    @pl.loop(1, early)
    def _(offset):
        peer = col_peer(offset)
        peak, total = row_stat(peer)
        stat_send[peer, 0:1, :] = peak
        stat_send[peer, 1:2, :] = total

    pl.semaphore_wait(barrier, n_col - 1 + n_row - 1)

    @pl.loop(1, early)
    def _(offset):
        to_owner(stat_send, stat_recv, stat_ss, stat_rs, col_peer(offset)).start()

    @pl.loop(early, n_col)
    def _(offset):
        peer = col_peer(offset)
        peak, total = row_stat(peer)
        stat_send[peer, 0:1, :] = peak
        stat_send[peer, 1:2, :] = total
        to_owner(stat_send, stat_recv, stat_ss, stat_rs, peer).start()

    @pl.loop(1, n_col)
    def _(offset):
        from_peer(stat_send, stat_recv, stat_ss, stat_rs, col_peer(offset)).wait()

    peaks = stat_recv[:, 0:1, :]
    top = jnp.max(peaks, axis=0, keepdims=True)
    row_total = jnp.sum(stat_recv[:, 1:2, :] * jnp.exp2(peaks - top), axis=0)
    own_mass = block_of(src_mass_ref, me)
    rp_all[me] = log2(own_mass) - (top[0] + log2(row_total))

    @pl.loop(1, n_col)
    def _(offset):
        spread(rp_all, rp_ss, rp_rs, col_peer(offset)).start()

    @pl.loop(1, n_col)
    def _(offset):
        spread_from(rp_all, rp_ss, rp_rs, col_peer(offset)).wait()

    strip = 64

    def folded(value, join):
        parts = [value[:, at : at + fold] for at in range(0, width, fold)]
        return functools.reduce(join, parts)

    @pl.loop(0, n_tgt // strip)
    def _(index):
        rows = pl.ds(pl.multiple_of(index * strip, strip), strip)

        def highest(block, running):
            return jnp.maximum(running, folded(score[block, rows, :] + rp_all[block], jnp.maximum))

        running = lax.fori_loop(0, n_col, highest, jnp.full((strip, fold), -3e38, jnp.float32), unroll=4)
        col_max[rows, :] = running
        peak = jnp.max(running, axis=1, keepdims=True)

        def summed(block, running):
            part = jnp.exp2(score[block, rows, :] + (rp_all[block] - peak))
            plan[block, rows, :] = part.astype(jnp.bfloat16)
            return running + folded(part, jnp.add)

        col_sum[rows, :] = lax.fori_loop(0, n_col, summed, jnp.zeros((strip, fold), jnp.float32), unroll=4)

    own_peak = jnp.max(col_max[...].T, axis=0, keepdims=True)
    col_stat[mine, 0:1, :] = own_peak
    col_stat[mine, 1:2, :] = jnp.sum(col_sum[...].T, axis=0, keepdims=True)

    @pl.loop(1, n_row)
    def _(offset):
        row_spread(col_stat, cs_ss, cs_rs, row_peer(offset)).start()

    @pl.loop(1, n_row)
    def _(offset):
        row_spread_from(col_stat, cs_ss, cs_rs, row_peer(offset)).wait()

    peaks = col_stat[:, 0:1, :]
    top = jnp.max(peaks, axis=0, keepdims=True)
    col_total = jnp.sum(col_stat[:, 1:2, :] * jnp.exp2(peaks - top), axis=0)
    tgt_mass = tgt_mass_ref[...]
    col_pot = log2(tgt_mass) - (top[0] + log2(col_total))
    gain = jnp.exp2(own_peak + col_pot)

    gain_rows = hi_lo_rows(gain)

    def row_sum(block):
        rows = jnp.dot(gain_rows, plan[block], preferred_element_type=jnp.float32)
        return rows[0:1] + rows[1:2]

    @pl.loop(1, n_col)
    def _(offset):
        peer = col_peer(offset)
        sum_send[peer] = row_sum(peer)
        to_owner(sum_send, sum_recv, sum_ss, sum_rs, peer).start()

    sum_recv[me] = row_sum(me)

    @pl.loop(1, n_col)
    def _(offset):
        from_peer(sum_send, sum_recv, sum_ss, sum_rs, col_peer(offset)).wait()

    u_all[me] = own_mass / jnp.sum(sum_recv[...], axis=0)

    @pl.loop(1, n_col)
    def _(offset):
        spread(u_all, u_ss, u_rs, col_peer(offset)).start()

    @pl.loop(1, n_col)
    def _(offset):
        spread_from(u_all, u_ss, u_rs, col_peer(offset)).wait()

    def col_add(block, running):
        return running + lax.dot_general(
            hi_lo_rows(u_all[block]), plan[block], (((1,), (1,)), ((), ())), preferred_element_type=jnp.float32
        )

    both = lax.fori_loop(0, n_col, col_add, jnp.zeros((NUM_ROWS, n_tgt), jnp.float32))
    col_part[mine] = gain * (both[0:1] + both[1:2])

    @pl.loop(1, n_row)
    def _(offset):
        row_spread(col_part, cp_ss, cp_rs, row_peer(offset)).start()

    for block in range(n_col):
        row_out[:, block * width : (block + 1) * width] = POT_SCALE * (rp_all[block] + log2(u_all[block]))

    @pl.loop(1, n_row)
    def _(offset):
        row_spread_from(col_part, cp_ss, cp_rs, row_peer(offset)).wait()

    ratio = tgt_mass / jnp.sum(col_part[...], axis=0)
    col_out[...] = POT_SCALE * (col_pot + log2(ratio))
    factor = gain * ratio
    weighted_high, weighted_low = hi_lo(desc_ref[...].astype(jnp.float32) * factor)
    weights = jnp.concatenate([weighted_high, hi_lo_rows(factor), weighted_low], axis=0)

    n_chip = n_col // 2
    chip = me // 2
    core = lax.rem(me, 2)

    def image(block):
        sums = jnp.dot(weights, plan[block], preferred_element_type=jnp.float32)
        den = sums[n_feat : n_feat + 1] + sums[n_feat + 1 : n_feat + 2]
        return sums[:n_feat] + sums[n_feat + NUM_ROWS :], den

    def to_pair(place):
        return pltpu.make_async_remote_copy(
            src_ref=pair_send.at[place], dst_ref=pair_recv.at[place],
            send_sem=pair_ss.at[place], recv_sem=pair_rs.at[place],
            device_id={"col": 2 * chip + 1 - core}, device_id_type=MESH,
        )

    def to_image(send, recv, ssem, rsem, place):
        return pltpu.make_async_remote_copy(
            src_ref=send.at[place], dst_ref=recv.at[chip], send_sem=ssem.at[place], recv_sem=rsem.at[chip],
            device_id={"col": 2 * place + core}, device_id_type=MESH,
        )

    def from_image(send, recv, ssem, rsem, place):
        return pltpu.make_async_remote_copy(
            src_ref=send.at[place], dst_ref=recv.at[place], send_sem=ssem.at[place], recv_sem=rsem.at[place],
            device_id={"col": 2 * place + core}, device_id_type=MESH,
        )

    def chip_peer(offset):
        return flipped(chip, n_chip - offset, n_chip)

    def pair_start(place):
        num, den = image(2 * place + 1 - core)
        pair_send[place, 0:n_feat, :] = num
        pair_send[place, n_feat:, :] = jnp.broadcast_to(den, (8, width))
        to_pair(place).start()

    @pl.loop(1, n_chip)
    def _(offset):
        pair_start(chip_peer(offset))

    pair_start(chip)

    def pair_total(place):
        num, den = image(2 * place + core)
        to_pair(place).wait()
        return num + pair_recv[place, 0:n_feat, :], den + pair_recv[place, n_feat : n_feat + 1, :]

    @pl.loop(1, n_chip)
    def _(offset):
        place = chip_peer(offset)
        num, den = pair_total(place)
        num_send[place] = num.astype(jnp.bfloat16)
        den_send[place] = den
        to_image(num_send, num_recv, num_ss, num_rs, place).start()
        to_image(den_send, den_recv, den_ss, den_rs, place).start()

    num, den = pair_total(chip)
    map_out[...] = num
    den_recv[chip] = den

    @pl.loop(1, n_chip)
    def _(offset):
        place = chip_peer(offset)
        from_image(num_send, num_recv, num_ss, num_rs, place).wait()
        from_image(den_send, den_recv, den_ss, den_rs, place).wait()
        map_out[...] += num_recv[place].astype(jnp.float32)

    map_out[...] = map_out[...] / jnp.sum(den_recv[...], axis=0)


def on_device(n_row, n_col, src_pos, src_desc, src_mass, tgt_pos, tgt_desc, tgt_mass, pattern):
    n_src = src_pos.shape[1]
    n_tgt = tgt_pos.shape[1]
    n_feat = src_desc.shape[0]
    tgt_clusters = n_tgt // CL
    width = n_src // n_col
    column = lax.axis_index("col")
    own = column * tgt_clusters + jnp.arange(tgt_clusters, dtype=jnp.int32)
    named = jnp.any(pattern[None, :, :] == own[:, None, None], axis=2)
    named = jnp.broadcast_to(named[:, :, None], named.shape + (CL,)).reshape(tgt_clusters, n_src)
    n_mask = -(-(4 + tgt_clusters) // 8) * 8 - 4
    src_mask = jnp.where(jnp.pad(named, ((0, n_mask - tgt_clusters), (0, 0)), constant_values=True), 0.0, MASKED)
    depth = n_feat + 6 * (4 + n_mask)

    def blocked(value):
        if width % 128 == 0:
            return value
        return value.reshape(value.shape[0], n_col, width).transpose(1, 0, 2)

    f32, bf16 = jnp.float32, jnp.bfloat16
    vmem = pl.BlockSpec(memory_space=pltpu.VMEM)
    fold = min(width, 128)
    dma = pltpu.SemaphoreType.DMA
    row_pot, col_pot, mapped = pl.pallas_call(
        functools.partial(kernel, n_row, n_col),
        out_shape=(
            jax.ShapeDtypeStruct((1, n_src), f32),
            jax.ShapeDtypeStruct((1, n_tgt), f32),
            jax.ShapeDtypeStruct((n_feat, width), f32),
        ),
        in_specs=[vmem] * 7,
        out_specs=(vmem, vmem, vmem),
        scratch_shapes=[
            pltpu.VMEM((depth, width), bf16),
            pltpu.VMEM((n_tgt, depth), bf16),
            pltpu.VMEM((n_col, n_tgt, width), f32),
            pltpu.VMEM((n_col, n_tgt, width), bf16),
            pltpu.VMEM((n_col, 2, width), f32),
            pltpu.VMEM((n_col, 2, width), f32),
            pltpu.VMEM((n_col, 1, width), f32),
            pltpu.VMEM((n_tgt, fold), f32),
            pltpu.VMEM((n_tgt, fold), f32),
            pltpu.VMEM((n_row, 2, n_tgt), f32),
            pltpu.VMEM((n_col, 1, width), f32),
            pltpu.VMEM((n_col, 1, width), f32),
            pltpu.VMEM((n_col, 1, width), f32),
            pltpu.VMEM((n_row, 1, n_tgt), f32),
            pltpu.VMEM((n_col // 2, n_feat + 8, width), f32),
            pltpu.VMEM((n_col // 2, n_feat + 8, width), f32),
            pltpu.VMEM((n_col // 2, n_feat, width), bf16),
            pltpu.VMEM((n_col // 2, n_feat, width), bf16),
            pltpu.VMEM((n_col // 2, 1, width), f32),
            pltpu.VMEM((n_col // 2, 1, width), f32),
            dma((n_col,)), dma((n_col,)),
            dma((n_col,)), dma((n_col,)),
            dma((n_row,)), dma((n_row,)),
            dma((n_col,)), dma((n_col,)),
            dma((n_col,)), dma((n_col,)),
            dma((n_row,)), dma((n_row,)),
            dma((n_col // 2,)), dma((n_col // 2,)),
            dma((n_col // 2,)), dma((n_col // 2,)),
            dma((n_col // 2,)), dma((n_col // 2,)),
        ],
        compiler_params=pltpu.CompilerParams(
            collective_id=0, has_side_effects=True, vmem_limit_bytes=56 * 1024 * 1024
        ),
    )(
        blocked(src_pos), blocked(src_desc), blocked(src_mask), blocked(src_mass.reshape(1, n_src)),
        tgt_pos, tgt_desc, tgt_mass.reshape(1, n_tgt),
    )
    return (row_pot.reshape(-1), col_pot.reshape(-1), mapped.T)


def solution(mesh):
    in_specs = (
        P(None, "row"),
        P(None, "row"),
        P("row"),
        P(None, "col"),
        P(None, "col"),
        P("col"),
        P("row", None),
    )
    out_specs = (P("row"), P("col"), P(("row", "col"), None))
    body = functools.partial(on_device, mesh.shape["row"], mesh.shape["col"])
    return jax.shard_map(body, mesh=mesh, in_specs=in_specs, out_specs=out_specs, check_vma=False)
```

```python
import functools
import math

import jax
import jax.numpy as jnp
from jax import lax
from jax.experimental import pallas as pl
from jax.experimental.pallas import tpu as pltpu
from jax.sharding import PartitionSpec as P

CL = 128
EPSILON = 0.05
LOG2E = 1.0 / math.log(2.0)
SCORE_SCALE = 2.0 * LOG2E / EPSILON
POT_SCALE = EPSILON * math.log(2.0)
MASKED = -(2.0**93)
MESH = pl.DeviceIdType.MESH
NUM_ROWS = 16


def log2(value):
    return jnp.log(value) * LOG2E


def float_parts(value):
    first = value.astype(jnp.bfloat16).astype(jnp.float32)
    rest = value - first
    second = rest.astype(jnp.bfloat16).astype(jnp.float32)
    return first, second, (rest - second).astype(jnp.bfloat16).astype(jnp.float32)


def hi_lo(value):
    high = value.astype(jnp.bfloat16)
    low = (value - high.astype(jnp.float32)).astype(jnp.bfloat16)
    return high, low


def hi_lo_rows(value):
    high = value.astype(jnp.bfloat16).astype(jnp.float32)
    low = value - high
    row = lax.broadcasted_iota(jnp.int32, (NUM_ROWS, value.shape[1]), 0)
    rows = jnp.where(row == 0, high, jnp.where(row == 1, low, 0.0))
    return rows.astype(jnp.bfloat16)


def flipped(place, mask, count):
    bits = count.bit_length() - 1
    if count != 1 << bits:
        return lax.rem(place + mask, count)
    digits = [lax.rem(lax.div(place, 1 << bit) + lax.div(mask, 1 << bit), 2) for bit in range(bits)]
    return sum(digit * (1 << bit) for bit, digit in enumerate(digits))


def kernel(
    n_row, n_col,
    src_pos_ref, src_desc_ref, pattern_ref, src_mass_ref, tgt_pos_ref, desc_ref, tgt_mass_ref,
    row_out, col_out, map_out,
    src_feat, tgt_feat, score, plan, stat_send, stat_recv, rp_all, col_max, col_sum, col_stat, sum_send, sum_recv, u_all,
    col_part, pair_send, pair_recv, num_send, num_recv, den_send, den_recv,
    stat_ss, stat_rs, rp_ss, rp_rs, cs_ss, cs_rs, sum_ss, sum_rs, u_ss, u_rs, cp_ss, cp_rs, pair_ss, pair_rs, num_ss, num_rs, den_ss, den_rs,
):
    me = lax.axis_index("col")
    mine = lax.axis_index("row")
    n_tgt = desc_ref.shape[1]
    width = map_out.shape[1]
    fold = min(width, 128)
    n_feat = desc_ref.shape[0]

    def col_peer(offset):
        return flipped(me, n_col - offset, n_col)

    def row_peer(offset):
        return lax.rem(mine + offset, n_row)

    barrier = pltpu.get_barrier_semaphore()

    @pl.loop(1, n_col)
    def _(offset):
        pl.semaphore_signal(barrier, inc=1, device_id={"col": col_peer(offset)}, device_id_type=MESH)

    @pl.loop(1, n_row)
    def _(offset):
        pl.semaphore_signal(barrier, inc=1, device_id={"row": row_peer(offset)}, device_id_type=MESH)

    def to_owner(send, recv, ssem, rsem, peer):
        return pltpu.make_async_remote_copy(
            src_ref=send.at[peer], dst_ref=recv.at[me], send_sem=ssem.at[peer], recv_sem=rsem.at[me],
            device_id={"col": peer}, device_id_type=MESH,
        )

    def from_peer(send, recv, ssem, rsem, peer):
        return pltpu.make_async_remote_copy(
            src_ref=send.at[peer], dst_ref=recv.at[peer], send_sem=ssem.at[peer], recv_sem=rsem.at[peer],
            device_id={"col": peer}, device_id_type=MESH,
        )

    def spread(buf, ssem, rsem, peer):
        return pltpu.make_async_remote_copy(
            src_ref=buf.at[me], dst_ref=buf.at[me], send_sem=ssem.at[peer], recv_sem=rsem.at[me],
            device_id={"col": peer}, device_id_type=MESH,
        )

    def spread_from(buf, ssem, rsem, peer):
        return pltpu.make_async_remote_copy(
            src_ref=buf.at[me], dst_ref=buf.at[peer], send_sem=ssem.at[peer], recv_sem=rsem.at[peer],
            device_id={"col": peer}, device_id_type=MESH,
        )

    def row_spread(buf, ssem, rsem, peer):
        return pltpu.make_async_remote_copy(
            src_ref=buf.at[mine], dst_ref=buf.at[mine], send_sem=ssem.at[peer], recv_sem=rsem.at[mine],
            device_id={"row": peer}, device_id_type=MESH,
        )

    def row_spread_from(buf, ssem, rsem, peer):
        return pltpu.make_async_remote_copy(
            src_ref=buf.at[mine], dst_ref=buf.at[peer], send_sem=ssem.at[peer], recv_sem=rsem.at[peer],
            device_id={"row": peer}, device_id_type=MESH,
        )

    def block_of(ref, block):
        if ref.ndim == 3:
            return ref[block]
        return ref[:, pl.ds(pl.multiple_of(block * width, 128), width)]

    desc32 = desc_ref[...].astype(jnp.float32)
    tgt_pos = tgt_pos_ref[...]
    norm = jnp.sum(tgt_pos * tgt_pos, axis=0, keepdims=True) + jnp.sum(desc32 * desc32, axis=0, keepdims=True)
    t1, t2, t3 = float_parts(jnp.concatenate([tgt_pos, -0.5 * norm], axis=0))
    upper = n_feat + 24
    tgt_feat[:, 0:upper] = jnp.concatenate([desc32, t1, t2, t1, t2, t3, t1], axis=0).T.astype(jnp.bfloat16)
    pattern = pattern_ref[...]
    n_cluster = pattern.shape[1]
    for place in range(n_tgt // CL):
        hits = jnp.where(pattern == me * (n_tgt // CL) + place, 1.0, 0.0)
        mask = jnp.where(jnp.max(hits, axis=0, keepdims=True) > 0.5, 0.0, MASKED)
        tgt_feat[place * CL : (place + 1) * CL, upper:] = jnp.broadcast_to(mask, (CL, n_cluster)).astype(jnp.bfloat16)
    source = lax.broadcasted_iota(jnp.int32, (n_cluster, width), 1)
    cluster = lax.broadcasted_iota(jnp.int32, (n_cluster, width), 0) * CL
    ones = jnp.ones((1, width), jnp.float32)

    def row_stat(block):
        s1, s2, s3 = float_parts(
            jnp.concatenate([block_of(src_pos_ref, block), ones], axis=0)
        )
        past = source + block * width - cluster
        in_cluster = jnp.where((past >= 0) & (past < CL), 1.0, 0.0)
        src_feat[0:n_feat, :] = block_of(src_desc_ref, block)
        src_feat[n_feat:, :] = jnp.concatenate([s1, s1, s2, s2, s1, s3, in_cluster], axis=0).astype(jnp.bfloat16)
        score[block] = SCORE_SCALE * jnp.dot(
            tgt_feat[...], src_feat[...], preferred_element_type=jnp.float32
        )
        peak = jnp.max(score[block], axis=0, keepdims=True)
        total = jnp.sum(jnp.exp2(score[block] - peak), axis=0, keepdims=True)
        return peak, total

    peak, total = row_stat(me)
    stat_recv[me, 0:1, :] = peak
    stat_recv[me, 1:2, :] = total
    early = n_col // 2

    @pl.loop(1, early)
    def _(offset):
        peer = col_peer(offset)
        peak, total = row_stat(peer)
        stat_send[peer, 0:1, :] = peak
        stat_send[peer, 1:2, :] = total

    pl.semaphore_wait(barrier, n_col - 1 + n_row - 1)

    @pl.loop(1, early)
    def _(offset):
        to_owner(stat_send, stat_recv, stat_ss, stat_rs, col_peer(offset)).start()

    @pl.loop(early, n_col)
    def _(offset):
        peer = col_peer(offset)
        peak, total = row_stat(peer)
        stat_send[peer, 0:1, :] = peak
        stat_send[peer, 1:2, :] = total
        to_owner(stat_send, stat_recv, stat_ss, stat_rs, peer).start()

    @pl.loop(1, n_col)
    def _(offset):
        from_peer(stat_send, stat_recv, stat_ss, stat_rs, col_peer(offset)).wait()

    peaks = stat_recv[:, 0:1, :]
    top = jnp.max(peaks, axis=0, keepdims=True)
    row_total = jnp.sum(stat_recv[:, 1:2, :] * jnp.exp2(peaks - top), axis=0)
    own_mass = block_of(src_mass_ref, me)
    rp_all[me] = log2(own_mass) - (top[0] + log2(row_total))

    @pl.loop(1, n_col)
    def _(offset):
        spread(rp_all, rp_ss, rp_rs, col_peer(offset)).start()

    @pl.loop(1, n_col)
    def _(offset):
        spread_from(rp_all, rp_ss, rp_rs, col_peer(offset)).wait()

    strip = 64

    def folded(value, join):
        parts = [value[:, at : at + fold] for at in range(0, width, fold)]
        return functools.reduce(join, parts)

    @pl.loop(0, n_tgt // strip)
    def _(index):
        rows = pl.ds(pl.multiple_of(index * strip, strip), strip)

        def highest(block, running):
            return jnp.maximum(running, folded(score[block, rows, :] + rp_all[block], jnp.maximum))

        running = lax.fori_loop(0, n_col, highest, jnp.full((strip, fold), -3e38, jnp.float32), unroll=4)
        col_max[rows, :] = running
        peak = jnp.max(running, axis=1, keepdims=True)

        def summed(block, running):
            part = jnp.exp2(score[block, rows, :] + (rp_all[block] - peak))
            plan[block, rows, :] = part.astype(jnp.bfloat16)
            return running + folded(part, jnp.add)

        col_sum[rows, :] = lax.fori_loop(0, n_col, summed, jnp.zeros((strip, fold), jnp.float32), unroll=4)

    own_peak = jnp.max(col_max[...].T, axis=0, keepdims=True)
    col_stat[mine, 0:1, :] = own_peak
    col_stat[mine, 1:2, :] = jnp.sum(col_sum[...].T, axis=0, keepdims=True)

    @pl.loop(1, n_row)
    def _(offset):
        row_spread(col_stat, cs_ss, cs_rs, row_peer(offset)).start()

    @pl.loop(1, n_row)
    def _(offset):
        row_spread_from(col_stat, cs_ss, cs_rs, row_peer(offset)).wait()

    peaks = col_stat[:, 0:1, :]
    top = jnp.max(peaks, axis=0, keepdims=True)
    col_total = jnp.sum(col_stat[:, 1:2, :] * jnp.exp2(peaks - top), axis=0)
    tgt_mass = tgt_mass_ref[...]
    col_pot = log2(tgt_mass) - (top[0] + log2(col_total))
    gain = jnp.exp2(own_peak + col_pot)

    gain_rows = hi_lo_rows(gain)

    def row_sum(block):
        rows = jnp.dot(gain_rows, plan[block], preferred_element_type=jnp.float32)
        return rows[0:1] + rows[1:2]

    @pl.loop(1, n_col)
    def _(offset):
        peer = col_peer(offset)
        sum_send[peer] = row_sum(peer)
        to_owner(sum_send, sum_recv, sum_ss, sum_rs, peer).start()

    sum_recv[me] = row_sum(me)

    @pl.loop(1, n_col)
    def _(offset):
        from_peer(sum_send, sum_recv, sum_ss, sum_rs, col_peer(offset)).wait()

    u_all[me] = own_mass / jnp.sum(sum_recv[...], axis=0)

    @pl.loop(1, n_col)
    def _(offset):
        spread(u_all, u_ss, u_rs, col_peer(offset)).start()

    @pl.loop(1, n_col)
    def _(offset):
        spread_from(u_all, u_ss, u_rs, col_peer(offset)).wait()

    def col_add(block, running):
        return running + lax.dot_general(
            hi_lo_rows(u_all[block]), plan[block], (((1,), (1,)), ((), ())), preferred_element_type=jnp.float32
        )

    both = lax.fori_loop(0, n_col, col_add, jnp.zeros((NUM_ROWS, n_tgt), jnp.float32))
    col_part[mine] = gain * (both[0:1] + both[1:2])

    @pl.loop(1, n_row)
    def _(offset):
        row_spread(col_part, cp_ss, cp_rs, row_peer(offset)).start()

    for block in range(n_col):
        row_out[:, block * width : (block + 1) * width] = POT_SCALE * (rp_all[block] + log2(u_all[block]))

    @pl.loop(1, n_row)
    def _(offset):
        row_spread_from(col_part, cp_ss, cp_rs, row_peer(offset)).wait()

    ratio = tgt_mass / jnp.sum(col_part[...], axis=0)
    col_out[...] = POT_SCALE * (col_pot + log2(ratio))
    factor = gain * ratio
    weighted_high, weighted_low = hi_lo(desc_ref[...].astype(jnp.float32) * factor)
    weights = jnp.concatenate([weighted_high, hi_lo_rows(factor), weighted_low], axis=0)

    n_chip = n_col // 2
    chip = me // 2
    core = lax.rem(me, 2)

    def image(block):
        sums = jnp.dot(weights, plan[block], preferred_element_type=jnp.float32)
        den = sums[n_feat : n_feat + 1] + sums[n_feat + 1 : n_feat + 2]
        return sums[:n_feat] + sums[n_feat + NUM_ROWS :], den

    def to_pair(place):
        return pltpu.make_async_remote_copy(
            src_ref=pair_send.at[place], dst_ref=pair_recv.at[place],
            send_sem=pair_ss.at[place], recv_sem=pair_rs.at[place],
            device_id={"col": 2 * chip + 1 - core}, device_id_type=MESH,
        )

    def to_image(send, recv, ssem, rsem, place):
        return pltpu.make_async_remote_copy(
            src_ref=send.at[place], dst_ref=recv.at[chip], send_sem=ssem.at[place], recv_sem=rsem.at[chip],
            device_id={"col": 2 * place + core}, device_id_type=MESH,
        )

    def from_image(send, recv, ssem, rsem, place):
        return pltpu.make_async_remote_copy(
            src_ref=send.at[place], dst_ref=recv.at[place], send_sem=ssem.at[place], recv_sem=rsem.at[place],
            device_id={"col": 2 * place + core}, device_id_type=MESH,
        )

    def chip_peer(offset):
        return flipped(chip, n_chip - offset, n_chip)

    def pair_start(place):
        num, den = image(2 * place + 1 - core)
        pair_send[place, 0:n_feat, :] = num
        pair_send[place, n_feat:, :] = jnp.broadcast_to(den, (8, width))
        to_pair(place).start()

    @pl.loop(1, n_chip)
    def _(offset):
        pair_start(chip_peer(offset))

    pair_start(chip)

    def pair_total(place):
        num, den = image(2 * place + core)
        to_pair(place).wait()
        return num + pair_recv[place, 0:n_feat, :], den + pair_recv[place, n_feat : n_feat + 1, :]

    @pl.loop(1, n_chip)
    def _(offset):
        place = chip_peer(offset)
        num, den = pair_total(place)
        num_send[place] = num.astype(jnp.bfloat16)
        den_send[place] = den
        to_image(num_send, num_recv, num_ss, num_rs, place).start()
        to_image(den_send, den_recv, den_ss, den_rs, place).start()

    num, den = pair_total(chip)
    map_out[...] = num
    den_recv[chip] = den

    @pl.loop(1, n_chip)
    def _(offset):
        place = chip_peer(offset)
        from_image(num_send, num_recv, num_ss, num_rs, place).wait()
        from_image(den_send, den_recv, den_ss, den_rs, place).wait()
        map_out[...] += num_recv[place].astype(jnp.float32)

    map_out[...] = map_out[...] / jnp.sum(den_recv[...], axis=0)


def hand_out(row_in, col_in, map_in, row_out, col_out, map_out):
    row_out[...] = row_in[...]
    col_out[...] = col_in[...]
    map_out[...] = map_in[...]


def on_device(n_row, n_col, src_pos, src_desc, src_mass, tgt_pos, tgt_desc, tgt_mass, pattern):
    n_src = src_pos.shape[1]
    n_tgt = tgt_pos.shape[1]
    n_feat = src_desc.shape[0]
    width = n_src // n_col
    depth = n_feat + 24 + pattern.shape[0]

    def blocked(value):
        if width % 128 == 0:
            return value
        return value.reshape(value.shape[0], n_col, width).transpose(1, 0, 2)

    f32, bf16 = jnp.float32, jnp.bfloat16
    vmem = pl.BlockSpec(memory_space=pltpu.VMEM)
    fold = min(width, 128)
    dma = pltpu.SemaphoreType.DMA
    row_pot, col_pot, mapped = pl.pallas_call(
        functools.partial(kernel, n_row, n_col),
        out_shape=(
            jax.ShapeDtypeStruct((1, n_src), f32),
            jax.ShapeDtypeStruct((1, n_tgt), f32),
            jax.ShapeDtypeStruct((n_feat, width), f32),
        ),
        in_specs=[vmem] * 7,
        out_specs=(vmem, vmem, vmem),
        scratch_shapes=[
            pltpu.VMEM((depth, width), bf16),
            pltpu.VMEM((n_tgt, depth), bf16),
            pltpu.VMEM((n_col, n_tgt, width), f32),
            pltpu.VMEM((n_col, n_tgt, width), bf16),
            pltpu.VMEM((n_col, 2, width), f32),
            pltpu.VMEM((n_col, 2, width), f32),
            pltpu.VMEM((n_col, 1, width), f32),
            pltpu.VMEM((n_tgt, fold), f32),
            pltpu.VMEM((n_tgt, fold), f32),
            pltpu.VMEM((n_row, 2, n_tgt), f32),
            pltpu.VMEM((n_col, 1, width), f32),
            pltpu.VMEM((n_col, 1, width), f32),
            pltpu.VMEM((n_col, 1, width), f32),
            pltpu.VMEM((n_row, 1, n_tgt), f32),
            pltpu.VMEM((n_col // 2, n_feat + 8, width), f32),
            pltpu.VMEM((n_col // 2, n_feat + 8, width), f32),
            pltpu.VMEM((n_col // 2, n_feat, width), bf16),
            pltpu.VMEM((n_col // 2, n_feat, width), bf16),
            pltpu.VMEM((n_col // 2, 1, width), f32),
            pltpu.VMEM((n_col // 2, 1, width), f32),
            dma((n_col,)), dma((n_col,)),
            dma((n_col,)), dma((n_col,)),
            dma((n_row,)), dma((n_row,)),
            dma((n_col,)), dma((n_col,)),
            dma((n_col,)), dma((n_col,)),
            dma((n_row,)), dma((n_row,)),
            dma((n_col // 2,)), dma((n_col // 2,)),
            dma((n_col // 2,)), dma((n_col // 2,)),
            dma((n_col // 2,)), dma((n_col // 2,)),
        ],
        compiler_params=pltpu.CompilerParams(
            collective_id=0, has_side_effects=True, vmem_limit_bytes=56 * 1024 * 1024
        ),
    )(
        blocked(src_pos), blocked(src_desc), pattern.T, blocked(src_mass.reshape(1, n_src)),
        tgt_pos, tgt_desc, tgt_mass.reshape(1, n_tgt),
    )
    row_pot, col_pot, mapped = pl.pallas_call(
        hand_out,
        out_shape=tuple(jax.ShapeDtypeStruct(value.shape, f32) for value in (row_pot, col_pot, mapped)),
        in_specs=[vmem] * 3,
        out_specs=(vmem, vmem, vmem),
        compiler_params=pltpu.CompilerParams(vmem_limit_bytes=4 * 1024 * 1024),
    )(row_pot, col_pot, mapped)
    return (row_pot.reshape(-1), col_pot.reshape(-1), mapped.T)


def solution(mesh):
    in_specs = (
        P(None, "row"),
        P(None, "row"),
        P("row"),
        P(None, "col"),
        P(None, "col"),
        P("col"),
        P("row", None),
    )
    out_specs = (P("row"), P("col"), P(("row", "col"), None))
    body = functools.partial(on_device, mesh.shape["row"], mesh.shape["col"])
    return jax.shard_map(body, mesh=mesh, in_specs=in_specs, out_specs=out_specs, check_vma=False)
```

```python
import functools
import math

import jax
import jax.numpy as jnp
from jax import lax
from jax.experimental import pallas as pl
from jax.experimental.pallas import tpu as pltpu
from jax.sharding import PartitionSpec as P

CL = 128
EPSILON = 0.05
LOG2E = 1.0 / math.log(2.0)
SCORE_SCALE = 2.0 * LOG2E / EPSILON
POT_SCALE = EPSILON * math.log(2.0)
MASKED = -(2.0**93)
MESH = pl.DeviceIdType.MESH
NUM_ROWS = 16


def log2(value):
    return jnp.log(value) * LOG2E


def float_parts(value):
    first = value.astype(jnp.bfloat16).astype(jnp.float32)
    rest = value - first
    second = rest.astype(jnp.bfloat16).astype(jnp.float32)
    return first, second, (rest - second).astype(jnp.bfloat16).astype(jnp.float32)


def hi_lo(value):
    high = value.astype(jnp.bfloat16)
    low = (value - high.astype(jnp.float32)).astype(jnp.bfloat16)
    return high, low


def hi_lo_rows(value):
    high = value.astype(jnp.bfloat16).astype(jnp.float32)
    low = value - high
    row = lax.broadcasted_iota(jnp.int32, (NUM_ROWS, value.shape[1]), 0)
    rows = jnp.where(row == 0, high, jnp.where(row == 1, low, 0.0))
    return rows.astype(jnp.bfloat16)


def flipped(place, mask, count):
    bits = count.bit_length() - 1
    if count != 1 << bits:
        return lax.rem(place + mask, count)
    digits = [lax.rem(lax.div(place, 1 << bit) + lax.div(mask, 1 << bit), 2) for bit in range(bits)]
    return sum(digit * (1 << bit) for bit, digit in enumerate(digits))


def kernel(
    n_row, n_col,
    src_pos_ref, src_desc_ref, pattern_ref, src_mass_ref, tgt_pos_ref, desc_ref, tgt_mass_ref,
    row_out, col_out, map_out,
    src_feat, tgt_feat, score, plan, stat_send, stat_recv, rp_all, col_max, col_sum, col_stat, sum_send, sum_recv, u_all,
    col_part, pair_send, pair_recv, num_send, num_recv, den_send, den_recv,
    stat_ss, stat_rs, rp_ss, rp_rs, cs_ss, cs_rs, sum_ss, sum_rs, u_ss, u_rs, cp_ss, cp_rs, pair_ss, pair_rs, num_ss, num_rs, den_ss, den_rs,
):
    me = lax.axis_index("col")
    mine = lax.axis_index("row")
    n_tgt = desc_ref.shape[1]
    width = map_out.shape[1]
    fold = min(width, 128)
    n_feat = desc_ref.shape[0]

    def col_peer(offset):
        return flipped(me, n_col - offset, n_col)

    def row_peer(offset):
        return lax.rem(mine + offset, n_row)

    barrier = pltpu.get_barrier_semaphore()

    @pl.loop(1, n_col)
    def _(offset):
        pl.semaphore_signal(barrier, inc=1, device_id={"col": col_peer(offset)}, device_id_type=MESH)

    @pl.loop(1, n_row)
    def _(offset):
        pl.semaphore_signal(barrier, inc=1, device_id={"row": row_peer(offset)}, device_id_type=MESH)

    def to_owner(send, recv, ssem, rsem, peer):
        return pltpu.make_async_remote_copy(
            src_ref=send.at[peer], dst_ref=recv.at[me], send_sem=ssem.at[0], recv_sem=rsem.at[0],
            device_id={"col": peer}, device_id_type=MESH,
        )

    def spread(buf, ssem, rsem, peer):
        return pltpu.make_async_remote_copy(
            src_ref=buf.at[me], dst_ref=buf.at[me], send_sem=ssem.at[0], recv_sem=rsem.at[0],
            device_id={"col": peer}, device_id_type=MESH,
        )

    def wait_all(send, recv, ssem, rsem):
        pltpu.make_async_remote_copy(
            src_ref=send.at[pl.ds(0, n_col - 1)], dst_ref=recv.at[pl.ds(0, n_col - 1)],
            send_sem=ssem.at[0], recv_sem=rsem.at[0],
            device_id={"col": lax.rem(me + 1, n_col)}, device_id_type=MESH,
        ).wait()

    def row_spread(buf, ssem, rsem, peer):
        return pltpu.make_async_remote_copy(
            src_ref=buf.at[mine], dst_ref=buf.at[mine], send_sem=ssem.at[peer], recv_sem=rsem.at[mine],
            device_id={"row": peer}, device_id_type=MESH,
        )

    def row_spread_from(buf, ssem, rsem, peer):
        return pltpu.make_async_remote_copy(
            src_ref=buf.at[mine], dst_ref=buf.at[peer], send_sem=ssem.at[peer], recv_sem=rsem.at[peer],
            device_id={"row": peer}, device_id_type=MESH,
        )

    def block_of(ref, block):
        if ref.ndim == 3:
            return ref[block]
        return ref[:, pl.ds(pl.multiple_of(block * width, 128), width)]

    desc32 = desc_ref[...].astype(jnp.float32)
    tgt_pos = tgt_pos_ref[...]
    norm = jnp.sum(tgt_pos * tgt_pos, axis=0, keepdims=True) + jnp.sum(desc32 * desc32, axis=0, keepdims=True)
    t1, t2, t3 = float_parts(jnp.concatenate([tgt_pos, -0.5 * norm], axis=0))
    upper = n_feat + 24
    tgt_feat[:, 0:upper] = jnp.concatenate([desc32, t1, t2, t1, t2, t3, t1], axis=0).T.astype(jnp.bfloat16)
    pattern = pattern_ref[...]
    n_cluster = pattern.shape[1]
    for place in range(n_tgt // CL):
        hits = jnp.where(pattern == me * (n_tgt // CL) + place, 1.0, 0.0)
        mask = jnp.where(jnp.max(hits, axis=0, keepdims=True) > 0.5, 0.0, MASKED)
        tgt_feat[place * CL : (place + 1) * CL, upper:] = jnp.broadcast_to(mask, (CL, n_cluster)).astype(jnp.bfloat16)
    source = lax.broadcasted_iota(jnp.int32, (n_cluster, width), 1)
    cluster = lax.broadcasted_iota(jnp.int32, (n_cluster, width), 0) * CL
    ones = jnp.ones((1, width), jnp.float32)

    def row_stat(block):
        s1, s2, s3 = float_parts(
            jnp.concatenate([block_of(src_pos_ref, block), ones], axis=0)
        )
        past = source + block * width - cluster
        in_cluster = jnp.where((past >= 0) & (past < CL), 1.0, 0.0)
        src_feat[0:n_feat, :] = block_of(src_desc_ref, block)
        src_feat[n_feat:, :] = jnp.concatenate([s1, s1, s2, s2, s1, s3, in_cluster], axis=0).astype(jnp.bfloat16)
        score[block] = SCORE_SCALE * jnp.dot(
            tgt_feat[...], src_feat[...], preferred_element_type=jnp.float32
        )
        peak = jnp.max(score[block], axis=0, keepdims=True)
        total = jnp.sum(jnp.exp2(score[block] - peak), axis=0, keepdims=True)
        return peak, total

    peak, total = row_stat(me)
    stat_recv[me, 0:1, :] = peak
    stat_recv[me, 1:2, :] = total
    early = n_col // 2

    @pl.loop(1, early)
    def _(offset):
        peer = col_peer(offset)
        peak, total = row_stat(peer)
        stat_send[peer, 0:1, :] = peak
        stat_send[peer, 1:2, :] = total

    pl.semaphore_wait(barrier, n_col - 1 + n_row - 1)

    @pl.loop(1, early)
    def _(offset):
        to_owner(stat_send, stat_recv, stat_ss, stat_rs, col_peer(offset)).start()

    @pl.loop(early, n_col)
    def _(offset):
        peer = col_peer(offset)
        peak, total = row_stat(peer)
        stat_send[peer, 0:1, :] = peak
        stat_send[peer, 1:2, :] = total
        to_owner(stat_send, stat_recv, stat_ss, stat_rs, peer).start()

    wait_all(stat_send, stat_recv, stat_ss, stat_rs)

    peaks = stat_recv[:, 0:1, :]
    top = jnp.max(peaks, axis=0, keepdims=True)
    row_total = jnp.sum(stat_recv[:, 1:2, :] * jnp.exp2(peaks - top), axis=0)
    own_mass = block_of(src_mass_ref, me)
    rp_all[me] = log2(own_mass) - (top[0] + log2(row_total))

    @pl.loop(1, n_col)
    def _(offset):
        spread(rp_all, rp_ss, rp_rs, col_peer(offset)).start()

    wait_all(rp_all, rp_all, rp_ss, rp_rs)

    strip = 64

    def folded(value, join):
        parts = [value[:, at : at + fold] for at in range(0, width, fold)]
        return functools.reduce(join, parts)

    @pl.loop(0, n_tgt // strip)
    def _(index):
        rows = pl.ds(pl.multiple_of(index * strip, strip), strip)

        def highest(block, running):
            return jnp.maximum(running, folded(score[block, rows, :] + rp_all[block], jnp.maximum))

        running = lax.fori_loop(0, n_col, highest, jnp.full((strip, fold), -3e38, jnp.float32), unroll=4)
        col_max[rows, :] = running
        peak = jnp.max(running, axis=1, keepdims=True)

        def summed(block, running):
            part = jnp.exp2(score[block, rows, :] + (rp_all[block] - peak))
            plan[block, rows, :] = part.astype(jnp.bfloat16)
            return running + folded(part, jnp.add)

        col_sum[rows, :] = lax.fori_loop(0, n_col, summed, jnp.zeros((strip, fold), jnp.float32), unroll=4)

    own_peak = jnp.max(col_max[...].T, axis=0, keepdims=True)
    col_stat[mine, 0:1, :] = own_peak
    col_stat[mine, 1:2, :] = jnp.sum(col_sum[...].T, axis=0, keepdims=True)

    @pl.loop(1, n_row)
    def _(offset):
        row_spread(col_stat, cs_ss, cs_rs, row_peer(offset)).start()

    @pl.loop(1, n_row)
    def _(offset):
        row_spread_from(col_stat, cs_ss, cs_rs, row_peer(offset)).wait()

    peaks = col_stat[:, 0:1, :]
    top = jnp.max(peaks, axis=0, keepdims=True)
    col_total = jnp.sum(col_stat[:, 1:2, :] * jnp.exp2(peaks - top), axis=0)
    tgt_mass = tgt_mass_ref[...]
    col_pot = log2(tgt_mass) - (top[0] + log2(col_total))
    gain = jnp.exp2(own_peak + col_pot)

    gain_rows = hi_lo_rows(gain)

    def row_sum(block):
        rows = jnp.dot(gain_rows, plan[block], preferred_element_type=jnp.float32)
        return rows[0:1] + rows[1:2]

    @pl.loop(1, n_col)
    def _(offset):
        peer = col_peer(offset)
        sum_send[peer] = row_sum(peer)
        to_owner(sum_send, sum_recv, sum_ss, sum_rs, peer).start()

    sum_recv[me] = row_sum(me)

    wait_all(sum_send, sum_recv, sum_ss, sum_rs)

    u_all[me] = own_mass / jnp.sum(sum_recv[...], axis=0)

    @pl.loop(1, n_col)
    def _(offset):
        spread(u_all, u_ss, u_rs, col_peer(offset)).start()

    wait_all(u_all, u_all, u_ss, u_rs)

    def col_add(block, running):
        return running + lax.dot_general(
            hi_lo_rows(u_all[block]), plan[block], (((1,), (1,)), ((), ())), preferred_element_type=jnp.float32
        )

    both = lax.fori_loop(0, n_col, col_add, jnp.zeros((NUM_ROWS, n_tgt), jnp.float32))
    col_part[mine] = gain * (both[0:1] + both[1:2])

    @pl.loop(1, n_row)
    def _(offset):
        row_spread(col_part, cp_ss, cp_rs, row_peer(offset)).start()

    for block in range(n_col):
        row_out[:, block * width : (block + 1) * width] = POT_SCALE * (rp_all[block] + log2(u_all[block]))

    @pl.loop(1, n_row)
    def _(offset):
        row_spread_from(col_part, cp_ss, cp_rs, row_peer(offset)).wait()

    ratio = tgt_mass / jnp.sum(col_part[...], axis=0)
    col_out[...] = POT_SCALE * (col_pot + log2(ratio))
    factor = gain * ratio
    weighted_high, weighted_low = hi_lo(desc_ref[...].astype(jnp.float32) * factor)
    weights = jnp.concatenate([weighted_high, hi_lo_rows(factor), weighted_low], axis=0)

    n_chip = n_col // 2
    chip = me // 2
    core = lax.rem(me, 2)

    def image(block):
        sums = jnp.dot(weights, plan[block], preferred_element_type=jnp.float32)
        den = sums[n_feat : n_feat + 1] + sums[n_feat + 1 : n_feat + 2]
        return sums[:n_feat] + sums[n_feat + NUM_ROWS :], den

    def to_pair(place):
        return pltpu.make_async_remote_copy(
            src_ref=pair_send.at[place], dst_ref=pair_recv.at[place],
            send_sem=pair_ss.at[place], recv_sem=pair_rs.at[place],
            device_id={"col": 2 * chip + 1 - core}, device_id_type=MESH,
        )

    def to_image(send, recv, ssem, rsem, place):
        return pltpu.make_async_remote_copy(
            src_ref=send.at[place], dst_ref=recv.at[chip], send_sem=ssem.at[place], recv_sem=rsem.at[chip],
            device_id={"col": 2 * place + core}, device_id_type=MESH,
        )

    def from_image(send, recv, ssem, rsem, place):
        return pltpu.make_async_remote_copy(
            src_ref=send.at[place], dst_ref=recv.at[place], send_sem=ssem.at[place], recv_sem=rsem.at[place],
            device_id={"col": 2 * place + core}, device_id_type=MESH,
        )

    def chip_peer(offset):
        return flipped(chip, n_chip - offset, n_chip)

    def pair_start(place):
        num, den = image(2 * place + 1 - core)
        pair_send[place, 0:n_feat, :] = num
        pair_send[place, n_feat:, :] = jnp.broadcast_to(den, (8, width))
        to_pair(place).start()

    @pl.loop(1, n_chip)
    def _(offset):
        pair_start(chip_peer(offset))

    pair_start(chip)

    def pair_total(place):
        num, den = image(2 * place + core)
        to_pair(place).wait()
        return num + pair_recv[place, 0:n_feat, :], den + pair_recv[place, n_feat : n_feat + 1, :]

    @pl.loop(1, n_chip)
    def _(offset):
        place = chip_peer(offset)
        num, den = pair_total(place)
        num_send[place] = num.astype(jnp.bfloat16)
        den_send[place] = den
        to_image(num_send, num_recv, num_ss, num_rs, place).start()
        to_image(den_send, den_recv, den_ss, den_rs, place).start()

    num, den = pair_total(chip)
    map_out[...] = num
    den_recv[chip] = den

    @pl.loop(1, n_chip)
    def _(offset):
        place = chip_peer(offset)
        from_image(num_send, num_recv, num_ss, num_rs, place).wait()
        from_image(den_send, den_recv, den_ss, den_rs, place).wait()
        map_out[...] += num_recv[place].astype(jnp.float32)

    map_out[...] = map_out[...] / jnp.sum(den_recv[...], axis=0)


def hand_out(row_in, col_in, map_in, row_out, col_out, map_out):
    row_out[...] = row_in[...]
    col_out[...] = col_in[...]
    map_out[...] = map_in[...]


def on_device(n_row, n_col, src_pos, src_desc, src_mass, tgt_pos, tgt_desc, tgt_mass, pattern):
    n_src = src_pos.shape[1]
    n_tgt = tgt_pos.shape[1]
    n_feat = src_desc.shape[0]
    width = n_src // n_col
    depth = n_feat + 24 + pattern.shape[0]

    def blocked(value):
        if width % 128 == 0:
            return value
        return value.reshape(value.shape[0], n_col, width).transpose(1, 0, 2)

    f32, bf16 = jnp.float32, jnp.bfloat16
    vmem = pl.BlockSpec(memory_space=pltpu.VMEM)
    fold = min(width, 128)
    dma = pltpu.SemaphoreType.DMA
    row_pot, col_pot, mapped = pl.pallas_call(
        functools.partial(kernel, n_row, n_col),
        out_shape=(
            jax.ShapeDtypeStruct((1, n_src), f32),
            jax.ShapeDtypeStruct((1, n_tgt), f32),
            jax.ShapeDtypeStruct((n_feat, width), f32),
        ),
        in_specs=[vmem] * 7,
        out_specs=(vmem, vmem, vmem),
        scratch_shapes=[
            pltpu.VMEM((depth, width), bf16),
            pltpu.VMEM((n_tgt, depth), bf16),
            pltpu.VMEM((n_col, n_tgt, width), f32),
            pltpu.VMEM((n_col, n_tgt, width), bf16),
            pltpu.VMEM((n_col, 2, width), f32),
            pltpu.VMEM((n_col, 2, width), f32),
            pltpu.VMEM((n_col, 1, width), f32),
            pltpu.VMEM((n_tgt, fold), f32),
            pltpu.VMEM((n_tgt, fold), f32),
            pltpu.VMEM((n_row, 2, n_tgt), f32),
            pltpu.VMEM((n_col, 1, width), f32),
            pltpu.VMEM((n_col, 1, width), f32),
            pltpu.VMEM((n_col, 1, width), f32),
            pltpu.VMEM((n_row, 1, n_tgt), f32),
            pltpu.VMEM((n_col // 2, n_feat + 8, width), f32),
            pltpu.VMEM((n_col // 2, n_feat + 8, width), f32),
            pltpu.VMEM((n_col // 2, n_feat, width), bf16),
            pltpu.VMEM((n_col // 2, n_feat, width), bf16),
            pltpu.VMEM((n_col // 2, 1, width), f32),
            pltpu.VMEM((n_col // 2, 1, width), f32),
            dma((1,)), dma((1,)),
            dma((1,)), dma((1,)),
            dma((n_row,)), dma((n_row,)),
            dma((1,)), dma((1,)),
            dma((1,)), dma((1,)),
            dma((n_row,)), dma((n_row,)),
            dma((n_col // 2,)), dma((n_col // 2,)),
            dma((n_col // 2,)), dma((n_col // 2,)),
            dma((n_col // 2,)), dma((n_col // 2,)),
        ],
        compiler_params=pltpu.CompilerParams(
            collective_id=0, has_side_effects=True, vmem_limit_bytes=56 * 1024 * 1024
        ),
    )(
        blocked(src_pos), blocked(src_desc), pattern.T, blocked(src_mass.reshape(1, n_src)),
        tgt_pos, tgt_desc, tgt_mass.reshape(1, n_tgt),
    )
    row_pot, col_pot, mapped = pl.pallas_call(
        hand_out,
        out_shape=tuple(jax.ShapeDtypeStruct(value.shape, f32) for value in (row_pot, col_pot, mapped)),
        in_specs=[vmem] * 3,
        out_specs=(vmem, vmem, vmem),
        compiler_params=pltpu.CompilerParams(vmem_limit_bytes=4 * 1024 * 1024),
    )(row_pot, col_pot, mapped)
    return (row_pot.reshape(-1), col_pot.reshape(-1), mapped.T)


def solution(mesh):
    in_specs = (
        P(None, "row"),
        P(None, "row"),
        P("row"),
        P(None, "col"),
        P(None, "col"),
        P("col"),
        P("row", None),
    )
    out_specs = (P("row"), P("col"), P(("row", "col"), None))
    body = functools.partial(on_device, mesh.shape["row"], mesh.shape["col"])
    return jax.shard_map(body, mesh=mesh, in_specs=in_specs, out_specs=out_specs, check_vma=False)
```
